32 devices in a mesh: groups: 2 (over x), seq: 16 (over z, y, core).
Axes of the slice: x: 2, y: 2, z: 4, core: 2. Of those that a mesh axis runs over, the one named last changes fastest.
Arguments:
- queries: bfloat16 [256, 2560], P(('groups', 'seq')), parts along dimension 0, may hold values from -160 to 160
- new_keys: bfloat16 [256, 2560], P(('groups', 'seq')), parts along dimension 0, may hold values from -7 to 7
- new_values: bfloat16 [256, 2560], P(('groups', 'seq')), parts along dimension 0, may hold values from -6 to 6
- cache_keys: bfloat16 [16384, 2560], P(('groups', 'seq')), parts along dimension 0, may hold values from -6 to 6
- cache_values: bfloat16 [16384, 2560], P(('groups', 'seq')), parts along dimension 0, may hold values from -6 to 6
- victims: int32 [32], P('groups'), parts along dimension 0, may hold values from 0 to 63, as said below
Outputs:
- attended: bfloat16 [256, 2560], P(('groups', 'seq')), parts along dimension 0
The draws below stay inside these ranges and needn't reach their ends.
There are 2 independent parts, one for each index of `groups`. The reference program is written for one: setup_inputs(seed, part) draws one part's arguments, and reference() takes and returns one part's arrays. A program takes and returns all parts, laid end to end along the dimension named above; each array names one. Nothing has to cross between parts.
Inputs may be any that keep to these rules, and one draw needn't show every extreme that they name: `victims`: 16 distinct block ids of the cache; the first and the last block are always among them.
All inputs are finite; a program needn't handle non-finite values.
Results may differ from the reference program's by a relative error of at most 0.01.
Values may be sent and summed in bfloat16 or wider, within the bound.
A program may use at most 128 MiB of HBM per device.

```python
import math
import jax
import jax.numpy as jnp
from jax import lax

H = 20
HD = 128
BLK = 128
TOK = 128
NBLK = 64
EVICT = 16


def drawn_pair(key):
    query_seed = jax.random.fold_in(key, 101)
    probe_seed = jax.random.fold_in(key, 202)
    columns = H * HD
    probe_rows = jax.random.truncated_normal(probe_seed, -6.0, 6.0, (TOK, columns), jnp.float32)
    query_rows = 3.0 * jax.random.truncated_normal(query_seed, -5.0, 5.0, (TOK, columns), jnp.float32)
    return (query_rows, probe_rows)


def draw_queries(key, part):
    return drawn_pair(key)[0].astype(jnp.bfloat16)


def draw_new_keys(key, part):
    return drawn_pair(key)[1].astype(jnp.bfloat16)


def draw_victims(key, part):
    middle = jax.random.permutation(jax.random.fold_in(key, 404), NBLK - 2).astype(jnp.int32) + 1
    ends = jnp.array([0, NBLK - 1]).astype(jnp.int32)
    chosen = jnp.concatenate([ends, middle[:EVICT - 2]])
    return jax.random.permutation(jax.random.fold_in(key, 505), chosen).astype(jnp.int32)


def block_levels(stream_key, extent, shards, smallest, top_value):
    def one(position, parts):
        steps = jax.random.uniform(jax.random.fold_in(jax.random.fold_in(stream_key, 6), position), (parts,), jnp.float32, smallest / len(shards), top_value / len(shards))
        return jnp.repeat(jnp.exp(steps), extent[position] // parts).reshape((-1,) + (1,) * (len(extent) - position - 1))

    factor_of = one(*shards[0])
    for cut in shards[1:]:
        factor_of = factor_of * one(*cut)
    return factor_of


def scatter_about(stream_key, dims, scale, reach, split=(), kind=jnp.bfloat16):
    values = jax.random.normal(stream_key, dims, jnp.float32) * scale
    if len(split) > 0:
        values = block_levels(stream_key, dims, split, -0.22, 0.18) * values
    return jnp.clip(values, min=-reach, max=reach).astype(kind)


def setup_inputs(seed: int = 0, part: int = 0) -> dict:
    streams_of = jax.random.split(jax.random.key(seed), 7)
    part_keys = jax.random.split(jax.random.fold_in(streams_of[6], part), 7)
    return {
        "queries": draw_queries(jax.random.fold_in(jax.random.fold_in(streams_of[6], part), 71), part),
        "new_keys": draw_new_keys(jax.random.fold_in(jax.random.fold_in(streams_of[6], part), 71), part),
        "new_values": scatter_about(part_keys[2], (TOK, H * HD), 1.0, 6.0, ((0, 16),)),
        "cache_keys": scatter_about(part_keys[3], (NBLK * BLK, H * HD), 1.0, 6.0, ((0, 16),)),
        "cache_values": scatter_about(part_keys[4], (NBLK * BLK, H * HD), 1.0, 6.0, ((0, 16),)),
        "victims": draw_victims(jax.random.fold_in(jax.random.fold_in(streams_of[6], part), 71), part),
    }


def similarity(query_cols, other):
    return lax.dot_general(query_cols, other, (((1,), (1,)), ((), ())), preferred_element_type=jnp.float32)

def reference(queries, new_keys, new_values, cache_keys, cache_values, victims):
    block_total = cache_keys.shape[0] // BLK
    evicted = jnp.zeros((block_total,), jnp.int32).at[victims].set(1)
    cache_live = jnp.repeat(evicted == 0, BLK)[None, :]
    scaling = 1.0 / math.sqrt(HD)

    def one_head(head):
        first_col = head * HD
        query_cols = lax.dynamic_slice_in_dim(queries, first_col, HD, 1)
        cached = similarity(query_cols, lax.dynamic_slice_in_dim(cache_keys, first_col, HD, 1)) * scaling
        cached = jnp.where(cache_live, cached, -1e+30)
        fresh_scores = similarity(query_cols, lax.dynamic_slice_in_dim(new_keys, first_col, HD, 1)) * scaling
        row_top = jnp.maximum(lax.optimization_barrier(jnp.max(cached, axis=1)), lax.optimization_barrier(jnp.max(fresh_scores, axis=1)))
        cached_exp = jnp.where(cache_live, jnp.exp(cached - row_top[:, None]), 0.0)
        fresh_exp = jnp.exp(fresh_scores - row_top[:, None])
        row_mass = lax.optimization_barrier(jnp.sum(cached_exp, axis=1)) + lax.optimization_barrier(jnp.sum(fresh_exp, axis=1))
        head_out = jnp.dot(cached_exp.astype(jnp.bfloat16), lax.dynamic_slice_in_dim(cache_values, first_col, HD, 1), preferred_element_type=jnp.float32)
        head_out = head_out + jnp.dot(fresh_exp.astype(jnp.bfloat16), lax.dynamic_slice_in_dim(new_values, first_col, HD, 1), preferred_element_type=jnp.float32)
        return head_out / row_mass[:, None]
    stacked = lax.map(one_head, jnp.arange(H, dtype=jnp.int32))
    return jnp.transpose(stacked, (1, 0, 2)).reshape(TOK, H * HD).astype(jnp.bfloat16)
```

```python
import functools
import math

import jax
import jax.numpy as jnp
from jax import lax
from jax.experimental import pallas as pl
from jax.experimental.pallas import tpu as pltpu
from jax.sharding import PartitionSpec as P

HD = 128
BLK = 128
LANES = 128
HALF = 32
ROW_TILE = 128
SIZES = (4, 6, 6, 4)
GROUPS = ((0, 1), (1, 2), (2, 4))
ORDER = ((0, 0), (0, 1), (0, 2), (1, 0), (1, 1), (2, 0), (1, 2), (2, 1), (3, 0), (2, 2), (3, 1), (2, 3), (3, 2), (4, 0), (3, 3), (4, 1), (4, 2), (4, 3), (5, 0), (5, 1), (5, 2), (5, 3))


def factors(members):
    fc = 2 if members % 2 == 0 else 1
    rest = members // fc
    fa = rest
    for cand in range(1, rest + 1):
        if rest % cand == 0 and cand * cand >= rest:
            fa = cand
            break
    return fa, rest // fa, fc


def chunks_of(heads):
    return SIZES


def kernel(
    dims, sizes, q_hbm, nk_hbm, nv_hbm, vic_hbm, ck_ref, cv_ref, o_ref,
    nk_ref, nv_ref, vic_ref, qall, kbuf, vbuf, live, acc, send_c, recv_c, send_b, recv_b, send_a, recv_a,
    load_sem, small_sem, send_sem, ga_sem, gb_sem, gc_sem, rr_sem,
):
    fa, fb, fc = dims
    members = fa * fb * fc
    tok, columns = q_hbm.shape
    heads = columns // HD
    chunks = len(sizes)
    starts = [sum(sizes[:j]) * HD for j in range(chunks + 1)]
    rows = ck_ref.shape[0]
    keys = kbuf.shape[0]
    block_count = rows // BLK
    exponent = math.log2(math.e) / math.sqrt(HD)

    me = lax.axis_index("seq")
    c = lax.rem(me, fc)
    b = lax.rem(lax.div(me, fc), fb)
    a = lax.div(me, fc * fb)

    def index(a_, b_, c_):
        return (a_ * fb + b_) * fc + c_

    def slot(a_, b_, c_):
        return (c_ * fb + b_) * fa + a_

    def partners(x, size):
        if size & (size - 1):
            return [lax.rem(x + d, size) for d in range(1, size)], [
                lax.rem(x + size - d, size) for d in range(1, size)
            ]
        found = []
        for d in reversed(range(1, size)):
            y = x
            bit = 1
            while bit <= d:
                if d & bit:
                    y = y + bit - 2 * bit * lax.rem(lax.div(y, bit), 2)
                bit *= 2
            found.append(y)
        return found, found

    a_peers, a_from = partners(a, fa)
    b_peers, b_from = partners(b, fb)
    c_peers, c_from = partners(c, fc)
    devices = (
        [index(p, b, c) for p in a_peers]
        + [index(a, p, c) for p in b_peers]
        + [index(a, b, p) for p in c_peers]
    )
    na, nb, nc = fa - 1, fb - 1, fc - 1

    def cols(g):
        low, high = GROUPS[g]
        return pl.ds(starts[low], starts[high] - starts[low])

    def packed(j, h=0):
        return starts[j] + j * LANES + h * HD

    def stat(j):
        return pl.ds(packed(j, sizes[j]), LANES)

    def body(j):
        return pl.ds(packed(j), sizes[j] * HD)

    def wcols(j):
        return pl.ds(packed(j), sizes[j] * HD + LANES)

    barrier = pltpu.get_barrier_semaphore()
    for dev in devices:
        pl.semaphore_signal(
            barrier, inc=1, device_id={"seq": dev}, device_id_type=pl.DeviceIdType.MESH
        )

    loads = [
        pltpu.make_async_copy(src, dst.at[pl.ds(0, rows)], load_sem.at[k])
        for k, (src, dst) in enumerate(((ck_ref, kbuf), (cv_ref, vbuf)))
    ]
    own_slot = slot(a, b, c)
    own = pltpu.make_async_copy(q_hbm, qall.at[own_slot], small_sem.at[0])
    small = [
        pltpu.make_async_copy(nk_hbm, nk_ref, small_sem.at[1]),
        pltpu.make_async_copy(nv_hbm, nv_ref, small_sem.at[2]),
        pltpu.make_async_copy(vic_hbm, vic_ref, small_sem.at[3]),
    ]
    own.start()
    for copy in small:
        copy.start()
    for copy in loads:
        copy.start()

    def remote(src, dst, out, into, target):
        return pltpu.make_async_remote_copy(
            src_ref=src,
            dst_ref=dst,
            send_sem=send_sem.at[out],
            recv_sem=into,
            device_id={"seq": target},
            device_id_type=pl.DeviceIdType.MESH,
        )

    def arrived(ref, sem):
        pltpu.make_async_copy(ref, ref, sem).wait()

    def gather_a(j):
        src = qall.at[own_slot, :, cols(j)]
        return [remote(src, src, 0, ga_sem.at[j, k], devices[k]) for k in range(na)]

    def gather_b(j, source):
        block = own_slot if source == 0 else slot(a_from[source - 1], b, c)
        src = qall.at[block, :, cols(j)]
        return [remote(src, src, 1, gb_sem.at[j, k], devices[na + k]) for k in range(nb)]

    def gather_c(j, column):
        at_b = b if column == 0 else b_from[column - 1]
        src = qall.at[pl.ds(slot(0, at_b, c), fa), :, cols(j)]
        return [remote(src, src, 2, gc_sem.at[j], devices[na + nb + k]) for k in range(nc)]

    with jax.named_scope('bar'):
        own.wait()
        pl.semaphore_wait(barrier, len(devices))
    for j in range(len(GROUPS)):
        for copy in gather_a(j):
            copy.start()
        for copy in gather_b(j, 0):
            copy.start()
    for copy in small:
        copy.wait()

    fresh = nk_ref[...].astype(jnp.float32)
    spare = jnp.concatenate([fresh, fresh], axis=0).astype(jnp.bfloat16)
    fresh = nv_ref[...].astype(jnp.float32)
    value = jnp.concatenate([fresh, jnp.zeros_like(fresh)], axis=0).astype(jnp.bfloat16)
    step = 2 * tok
    none = jnp.zeros((step, columns), jnp.bfloat16)
    first = lax.broadcasted_iota(jnp.int32, (step, LANES), 0)
    for at in range(rows, keys, step):
        here = pl.ds(at, step)
        kbuf[here, :] = spare
        vbuf[here, :] = value if at == rows else none
        live[here, :] = jnp.where(first < (tok if at == rows else 0), 1.0, 0.0).astype(jnp.bfloat16)

    victims = vic_ref[...]
    for copy in loads:
        copy.wait()
    for k in range(block_count):
        hit = jnp.where(victims == me * block_count + k, 1.0, 0.0)
        hit = jnp.max(hit, axis=1, keepdims=True)
        live[pl.ds(k * BLK, BLK), :] = jnp.broadcast_to(1.0 - hit, (BLK, LANES)).astype(jnp.bfloat16)
        gone = jnp.broadcast_to(hit, (step, LANES)) > 0.5

        @pl.loop(0, BLK // step)
        def _(r):
            here = pl.ds(pl.multiple_of(k * BLK + r * step, step), step)
            for col in range(0, columns, LANES):
                lanes = pl.ds(col, LANES)
                kbuf[here, lanes] = jnp.where(gone, spare[:, col : col + LANES], kbuf[here, lanes])
                vbuf[here, lanes] = jnp.where(gone, none[:, :LANES], vbuf[here, lanes])

    tile_slots = max(1, min(members, ROW_TILE // tok))
    tiles = members // tile_slots

    def lane_of(r):
        return lax.broadcasted_iota(jnp.int32, (r, LANES), 1)

    def compute(j):
        def tile(t):
            first = t * tile_slots
            r = tile_slots * tok
            lane = lane_of(r)

            def scores(h):
                col = starts[j] + h * HD
                col = col if isinstance(col, int) else pl.multiple_of(col, HD)
                q = qall[pl.ds(first, tile_slots), :, pl.ds(col, HD)]
                q = q.astype(jnp.float32).reshape(r, HD).astype(jnp.bfloat16)
                return lax.dot_general(
                    q, kbuf[:, pl.ds(col, HD)], (((1,), (1,)), ((), ())),
                    preferred_element_type=jnp.float32,
                )

            def head(h, stats, s):
                col = starts[j] + h * HD
                col = col if isinstance(col, int) else pl.multiple_of(col, HD)
                top = jnp.max(s, axis=1, keepdims=True) * exponent
                top = top.astype(jnp.bfloat16).astype(jnp.float32)
                e = jnp.exp2(s * exponent - top)
                out = jnp.dot(
                    e.astype(jnp.bfloat16),
                    jnp.concatenate([vbuf[:, pl.ds(col, HD)], live[...]], axis=1),
                    preferred_element_type=jnp.float32,
                )
                out, mass = out[:, :HD], out[:, HD:]
                at = packed(j) + h * HD
                at = at if isinstance(at, int) else pl.multiple_of(at, HD)
                acc[pl.ds(first, tile_slots), :, pl.ds(at, HD)] = out.reshape(tile_slots, tok, HD)
                stats = jnp.where(lane == h, top, stats)
                return jnp.where(lane == h + HALF, mass, stats)

            stats = jnp.zeros((r, LANES), jnp.float32)
            if tiles == 1:
                ahead = scores(0)
                for h in range(sizes[j]):
                    now, ahead = ahead, scores(h + 1) if h + 1 < sizes[j] else None
                    stats = head(h, stats, now)
            else:
                stats = lax.fori_loop(0, sizes[j], lambda h, st: head(h, st, scores(h)), stats)
            acc[pl.ds(first, tile_slots), :, stat(j)] = stats.reshape(
                tile_slots, tok, LANES
            )

        if tiles == 1:
            tile(0)
        else:
            pl.loop(0, tiles)(tile)

    def encode(stats):
        high = stats.astype(jnp.bfloat16).astype(jnp.float32)
        return (high + pltpu.roll(stats - high, HALF, 1)).astype(jnp.bfloat16)

    def decode(stats):
        low = pltpu.roll(stats, LANES - HALF, 1)
        return stats + jnp.where(lane_of(stats.shape[0]) < HALF, 0.0, low)

    def pack(first, count, buf, j):
        r = count * tok
        buf[:, :, body(j)] = acc[pl.ds(first, count), :, body(j)].astype(jnp.bfloat16)
        stats = acc[pl.ds(first, count), :, stat(j)].reshape(r, LANES)
        buf[:, :, stat(j)] = encode(stats).reshape(count, tok, LANES)

    def merge(first, count, parts, j, last=False):
        r = count * tok
        at = stat(j)
        lane = lane_of(r)
        stats = [acc[pl.ds(first, count), :, at].reshape(r, LANES)]
        for ref in parts:
            stats.append(decode(ref[:, :, at].astype(jnp.float32).reshape(r, LANES)))
        top = functools.reduce(jnp.maximum, stats)
        factor = [jnp.exp2(s - top) for s in stats]
        mass = sum(pltpu.roll(f, HALF, 1) * s for f, s in zip(factor, stats))
        if last:
            inverse = pltpu.roll(1.0 / jnp.where(lane < HALF, 1.0, mass), LANES - HALF, 1)
            factor = [f * inverse for f in factor]
        for h in range(sizes[j]):
            here = pl.ds(packed(j, h), HD)
            total = acc[pl.ds(first, count), :, here].reshape(r, HD) * factor[0][:, h : h + 1]
            for f, ref in zip(factor[1:], parts):
                total = total + ref[:, :, here].astype(jnp.float32).reshape(r, HD) * f[:, h : h + 1]
            if last:
                o_ref[:, pl.ds(starts[j] + h * HD, HD)] = total.astype(jnp.bfloat16)
            else:
                acc[pl.ds(first, count), :, here] = total.reshape(count, tok, HD)
        if not last:
            fused = jnp.where(lane < HALF, top, jnp.where(lane < 2 * HALF, mass, 0.0))
            acc[pl.ds(first, count), :, at] = fused.reshape(count, tok, LANES)

    def scatter_c(j):
        return [
            remote(
                send_c.at[k, :, :, wcols(j)], recv_c.at[k, :, :, wcols(j)], 5, rr_sem.at[j, 2],
                devices[na + nb + k],
            )
            for k in range(nc)
        ]

    def scatter_b(j):
        return [
            remote(
                send_b.at[k, :, :, wcols(j)], recv_b.at[k, :, :, wcols(j)], 4, rr_sem.at[j, 1],
                devices[na + k],
            )
            for k in range(nb)
        ]

    def scatter_a(j):
        return [
            remote(
                send_a.at[k, :, :, wcols(j)], recv_a.at[k, :, :, wcols(j)], 3, rr_sem.at[j, 0],
                devices[k],
            )
            for k in range(na)
        ]

    def stage_0(j):
        for source in range(1, fa):
            gather_a(j)[source - 1].wait_recv()
            for copy in gather_b(j, source):
                copy.start()
        for copy in gather_c(j, 0):
            copy.start()

    def stage_1(j):
        for column in range(1, fb):
            arrived(qall.at[pl.ds(0, fa), :, cols(j)], gb_sem.at[j, column - 1])
            for copy in gather_c(j, column):
                copy.start()

    def stage_2(j):
        for g, (low, _) in enumerate(GROUPS):
            if nc and low == j:
                arrived(qall.at[pl.ds(0, nc * fa * fb), :, cols(g)], gc_sem.at[g])
        compute(j)
        for k, copy in enumerate(scatter_c(j)):
            pack(slot(0, 0, c_peers[k]), fa * fb, send_c.at[k], j)
            copy.start()

    def stage_3(j):
        if nc:
            arrived(recv_c.at[:, :, :, wcols(j)], rr_sem.at[j, 2])
        received = [recv_c.at[k] for k in range(nc)]
        for k, copy in enumerate(scatter_b(j)):
            first = b_peers[k] * fa
            merge(slot(0, b_peers[k], c), fa, [x.at[pl.ds(first, fa)] for x in received], j)
            pack(slot(0, b_peers[k], c), fa, send_b.at[k], j)
            copy.start()
        merge(slot(0, b, c), fa, [x.at[pl.ds(b * fa, fa)] for x in received], j)

    def stage_4(j):
        if nb:
            arrived(recv_b.at[:, :, :, wcols(j)], rr_sem.at[j, 1])
        merge(slot(0, b, c), fa, [recv_b.at[k] for k in range(nb)], j)
        for k, copy in enumerate(scatter_a(j)):
            pack(slot(a_peers[k], b, c), 1, send_a.at[k], j)
            copy.start()

    def stage_5(j):
        if na:
            arrived(recv_a.at[:, :, :, wcols(j)], rr_sem.at[j, 0])
        merge(own_slot, 1, [recv_a.at[k] for k in range(na)], j, last=True)

    stages = (stage_0, stage_1, stage_2, stage_3, stage_4, stage_5)
    for number, j in ORDER:
        with jax.named_scope(f'st{number}_{j}'):
            stages[number](j)
    for k, (count, ref) in enumerate((
        (na, qall.at[pl.ds(0, na)]),
        (nb, qall.at[pl.ds(0, fa * nb)]),
        (nc, qall.at[pl.ds(0, fa * fb * nc)]),
        (na, send_a), (nb, send_b), (nc, send_c),
    )):
        if count:
            arrived(ref, send_sem.at[k])


def per_device(queries, new_keys, new_values, cache_keys, cache_values, victims):
    members = lax.axis_size("seq")
    dims = fa, fb, fc = factors(members)
    tok, columns = queries.shape
    heads = columns // HD
    sizes = chunks_of(heads)
    chunks = len(sizes)
    parts = len(GROUPS)
    rows = cache_keys.shape[0]
    keys = rows + -(-2 * tok // LANES) * LANES
    total = columns + chunks * LANES
    bf16 = jnp.bfloat16
    vmem = pl.BlockSpec(memory_space=pltpu.VMEM)
    hbm = pl.BlockSpec(memory_space=pl.ANY)
    return pl.pallas_call(
        functools.partial(kernel, dims, sizes),
        out_shape=pltpu.VMEM((tok, columns), bf16),
        in_specs=[hbm] * 6,
        out_specs=vmem,
        scratch_shapes=[
            pltpu.VMEM((tok, columns), bf16),
            pltpu.VMEM((tok, columns), bf16),
            pltpu.VMEM((1, victims.shape[0]), jnp.int32),
            pltpu.VMEM((members, tok, columns), bf16),
            pltpu.VMEM((keys, columns), bf16),
            pltpu.VMEM((keys, columns), bf16),
            pltpu.VMEM((keys, LANES), bf16),
            pltpu.VMEM((members, tok, total), jnp.float32),
            pltpu.VMEM((max(1, fc - 1), fa * fb, tok, total), bf16),
            pltpu.VMEM((max(1, fc - 1), fa * fb, tok, total), bf16),
            pltpu.VMEM((max(1, fb - 1), fa, tok, total), bf16),
            pltpu.VMEM((max(1, fb - 1), fa, tok, total), bf16),
            pltpu.VMEM((max(1, fa - 1), 1, tok, total), bf16),
            pltpu.VMEM((max(1, fa - 1), 1, tok, total), bf16),
            pltpu.SemaphoreType.DMA((2,)),
            pltpu.SemaphoreType.DMA((4,)),
            pltpu.SemaphoreType.DMA((6,)),
            pltpu.SemaphoreType.DMA((parts, max(1, fa - 1))),
            pltpu.SemaphoreType.DMA((parts, max(1, fb - 1))),
            pltpu.SemaphoreType.DMA((parts,)),
            pltpu.SemaphoreType.DMA((chunks, 3)),
        ],
        compiler_params=pltpu.CompilerParams(
            collective_id=0, has_side_effects=True, vmem_limit_bytes=60 * 1024 * 1024
        ),
    )(queries, new_keys, new_values, victims.reshape(1, -1), cache_keys, cache_values)


def solution(mesh):
    row = P(("groups", "seq"), None)
    return jax.shard_map(
        per_device,
        mesh=mesh,
        in_specs=(row, row, row, row, row, P("groups")),
        out_specs=row,
        check_vma=False,
    )
```

```python
import functools
import math

import jax
import jax.numpy as jnp
from jax import lax
from jax.experimental import pallas as pl
from jax.experimental.pallas import tpu as pltpu
from jax.sharding import PartitionSpec as P

HD = 128
BLK = 128
LANES = 128
HALF = 32
ROW_TILE = 128
CUTS = (0.15, 0.45, 0.8)


def factors(members):
    fc = 2 if members % 2 == 0 else 1
    rest = members // fc
    fa = rest
    for cand in range(1, rest + 1):
        if rest % cand == 0 and cand * cand >= rest:
            fa = cand
            break
    return fa, rest // fa, fc


def chunks_of(heads):
    bounds = sorted({0, heads, *(round(heads * cut) for cut in CUTS)})
    sizes = []
    for low, high in zip(bounds, bounds[1:]):
        while high - low > HALF:
            sizes.append(HALF)
            low += HALF
        sizes.append(high - low)
    return tuple(sizes)


def groups_of(chunks):
    bounds = sorted({0, min(1, chunks), min(2, chunks), chunks})
    return tuple(zip(bounds, bounds[1:]))


def order_of(chunks, groups):
    order = [(0, g) for g in range(groups)] + [(1, g) for g in range(min(2, groups))]
    for j in range(chunks):
        order.append((2, j))
        if j == 0:
            order += [(1, g) for g in range(2, groups)]
        else:
            order.append((3, j - 1))
    if chunks > 3:
        order.append((4, 0))
    order.append((3, chunks - 1))
    order += [(4, j) for j in range(chunks) if (4, j) not in order]
    return order + [(5, j) for j in range(chunks)]


def kernel(
    dims, sizes, q_hbm, nk_hbm, nv_hbm, vic_hbm, ck_ref, cv_ref, o_ref,
    nk_ref, nv_ref, vic_ref, qall, kbuf, vbuf, live, acc, send_c, recv_c, send_b, recv_b, send_a, recv_a,
    load_sem, small_sem, send_sem, ga_sem, gb_sem, gc_sem, rr_sem,
):
    fa, fb, fc = dims
    members = fa * fb * fc
    tok, columns = q_hbm.shape
    heads = columns // HD
    chunks = len(sizes)
    starts = [sum(sizes[:j]) * HD for j in range(chunks + 1)]
    groups = groups_of(chunks)
    rows = ck_ref.shape[0]
    keys = kbuf.shape[0]
    block_count = rows // BLK
    exponent = math.log2(math.e) / math.sqrt(HD)

    me = lax.axis_index("seq")
    c = lax.rem(me, fc)
    b = lax.rem(lax.div(me, fc), fb)
    a = lax.div(me, fc * fb)

    def index(a_, b_, c_):
        return (a_ * fb + b_) * fc + c_

    def slot(a_, b_, c_):
        return (c_ * fb + b_) * fa + a_

    def partners(x, size):
        if size & (size - 1):
            return [lax.rem(x + d, size) for d in range(1, size)], [
                lax.rem(x + size - d, size) for d in range(1, size)
            ]
        found = []
        for d in reversed(range(1, size)):
            y = x
            bit = 1
            while bit <= d:
                if d & bit:
                    y = y + bit - 2 * bit * lax.rem(lax.div(y, bit), 2)
                bit *= 2
            found.append(y)
        return found, found

    a_peers, a_from = partners(a, fa)
    b_peers, b_from = partners(b, fb)
    c_peers, c_from = partners(c, fc)
    devices = (
        [index(p, b, c) for p in a_peers]
        + [index(a, p, c) for p in b_peers]
        + [index(a, b, p) for p in c_peers]
    )
    na, nb, nc = fa - 1, fb - 1, fc - 1

    def cols(g):
        low, high = groups[g]
        return pl.ds(starts[low], starts[high] - starts[low])

    def packed(j, h=0):
        return starts[j] + j * LANES + h * HD

    def stat(j):
        return pl.ds(packed(j, sizes[j]), LANES)

    def body(j):
        return pl.ds(packed(j), sizes[j] * HD)

    def wcols(j):
        return pl.ds(packed(j), sizes[j] * HD + LANES)

    barrier = pltpu.get_barrier_semaphore()
    for dev in devices:
        pl.semaphore_signal(
            barrier, inc=1, device_id={"seq": dev}, device_id_type=pl.DeviceIdType.MESH
        )

    loads = [
        pltpu.make_async_copy(src, dst.at[pl.ds(0, rows)], load_sem.at[k])
        for k, (src, dst) in enumerate(((ck_ref, kbuf), (cv_ref, vbuf)))
    ]
    own_slot = slot(a, b, c)
    own = pltpu.make_async_copy(q_hbm, qall.at[own_slot], small_sem.at[0])
    small = [
        pltpu.make_async_copy(nk_hbm, nk_ref, small_sem.at[1]),
        pltpu.make_async_copy(nv_hbm, nv_ref, small_sem.at[2]),
        pltpu.make_async_copy(vic_hbm, vic_ref, small_sem.at[3]),
    ]
    own.start()
    for copy in small:
        copy.start()
    for copy in loads:
        copy.start()

    def remote(src, dst, out, into, target):
        return pltpu.make_async_remote_copy(
            src_ref=src,
            dst_ref=dst,
            send_sem=send_sem.at[out],
            recv_sem=into,
            device_id={"seq": target},
            device_id_type=pl.DeviceIdType.MESH,
        )

    def arrived(ref, sem):
        pltpu.make_async_copy(ref, ref, sem).wait()

    def gather_a(j):
        src = qall.at[own_slot, :, cols(j)]
        return [remote(src, src, 0, ga_sem.at[j, k], devices[k]) for k in range(na)]

    def gather_b(j, source):
        block = own_slot if source == 0 else slot(a_from[source - 1], b, c)
        src = qall.at[block, :, cols(j)]
        return [remote(src, src, 1, gb_sem.at[j, k], devices[na + k]) for k in range(nb)]

    def gather_c(j, column):
        at_b = b if column == 0 else b_from[column - 1]
        src = qall.at[pl.ds(slot(0, at_b, c), fa), :, cols(j)]
        return [remote(src, src, 2, gc_sem.at[j], devices[na + nb + k]) for k in range(nc)]

    own.wait()
    pl.semaphore_wait(barrier, len(devices))
    for j in range(len(groups)):
        for copy in gather_a(j):
            copy.start()
        for copy in gather_b(j, 0):
            copy.start()
    for copy in small:
        copy.wait()

    fresh = nk_ref[...].astype(jnp.float32)
    spare = jnp.concatenate([fresh, fresh], axis=0).astype(jnp.bfloat16)
    fresh = nv_ref[...].astype(jnp.float32)
    value = jnp.concatenate([fresh, jnp.zeros_like(fresh)], axis=0).astype(jnp.bfloat16)
    step = 2 * tok
    none = jnp.zeros((step, columns), jnp.bfloat16)
    first = lax.broadcasted_iota(jnp.int32, (step, LANES), 0)
    for at in range(rows, keys, step):
        here = pl.ds(at, step)
        kbuf[here, :] = spare
        vbuf[here, :] = value if at == rows else none
        live[here, :] = jnp.where(first < (tok if at == rows else 0), 1.0, 0.0).astype(jnp.bfloat16)

    victims = vic_ref[...]
    for copy in loads:
        copy.wait()
    for k in range(block_count):
        hit = jnp.where(victims == me * block_count + k, 1.0, 0.0)
        hit = jnp.max(hit, axis=1, keepdims=True)
        live[pl.ds(k * BLK, BLK), :] = jnp.broadcast_to(1.0 - hit, (BLK, LANES)).astype(jnp.bfloat16)
        gone = jnp.broadcast_to(hit, (step, LANES)) > 0.5

        @pl.loop(0, BLK // step)
        def _(r):
            here = pl.ds(pl.multiple_of(k * BLK + r * step, step), step)
            for col in range(0, columns, LANES):
                lanes = pl.ds(col, LANES)
                kbuf[here, lanes] = jnp.where(gone, spare[:, col : col + LANES], kbuf[here, lanes])
                vbuf[here, lanes] = jnp.where(gone, none[:, :LANES], vbuf[here, lanes])

    tile_slots = max(1, min(members, ROW_TILE // tok))
    tiles = members // tile_slots

    def lane_of(r):
        return lax.broadcasted_iota(jnp.int32, (r, LANES), 1)

    def compute(j):
        def tile(t):
            first = t * tile_slots
            r = tile_slots * tok
            lane = lane_of(r)

            def scores(h):
                col = starts[j] + h * HD
                col = col if isinstance(col, int) else pl.multiple_of(col, HD)
                q = qall[pl.ds(first, tile_slots), :, pl.ds(col, HD)]
                q = q.astype(jnp.float32).reshape(r, HD).astype(jnp.bfloat16)
                return lax.dot_general(
                    q, kbuf[:, pl.ds(col, HD)], (((1,), (1,)), ((), ())),
                    preferred_element_type=jnp.float32,
                )

            def head(h, stats, s):
                col = starts[j] + h * HD
                col = col if isinstance(col, int) else pl.multiple_of(col, HD)
                top = jnp.max(s, axis=1, keepdims=True) * exponent
                top = top.astype(jnp.bfloat16).astype(jnp.float32)
                e = jnp.exp2(s * exponent - top)
                out = jnp.dot(
                    e.astype(jnp.bfloat16),
                    jnp.concatenate([vbuf[:, pl.ds(col, HD)], live[...]], axis=1),
                    preferred_element_type=jnp.float32,
                )
                out, mass = out[:, :HD], out[:, HD:]
                at = packed(j) + h * HD
                at = at if isinstance(at, int) else pl.multiple_of(at, HD)
                acc[pl.ds(first, tile_slots), :, pl.ds(at, HD)] = out.reshape(tile_slots, tok, HD)
                stats = jnp.where(lane == h, top, stats)
                return jnp.where(lane == h + HALF, mass, stats)

            stats = jnp.zeros((r, LANES), jnp.float32)
            if tiles == 1:
                ahead = scores(0)
                for h in range(sizes[j]):
                    now, ahead = ahead, scores(h + 1) if h + 1 < sizes[j] else None
                    stats = head(h, stats, now)
            else:
                stats = lax.fori_loop(0, sizes[j], lambda h, st: head(h, st, scores(h)), stats)
            acc[pl.ds(first, tile_slots), :, stat(j)] = stats.reshape(
                tile_slots, tok, LANES
            )

        if tiles == 1:
            tile(0)
        else:
            pl.loop(0, tiles)(tile)

    def encode(stats):
        high = stats.astype(jnp.bfloat16).astype(jnp.float32)
        return (high + pltpu.roll(stats - high, HALF, 1)).astype(jnp.bfloat16)

    def decode(stats):
        low = pltpu.roll(stats, LANES - HALF, 1)
        return stats + jnp.where(lane_of(stats.shape[0]) < HALF, 0.0, low)

    def pack(first, count, buf, j):
        r = count * tok
        buf[:, :, body(j)] = acc[pl.ds(first, count), :, body(j)].astype(jnp.bfloat16)
        stats = acc[pl.ds(first, count), :, stat(j)].reshape(r, LANES)
        buf[:, :, stat(j)] = encode(stats).reshape(count, tok, LANES)

    def merge(first, count, parts, j, last=False):
        r = count * tok
        at = stat(j)
        lane = lane_of(r)
        stats = [acc[pl.ds(first, count), :, at].reshape(r, LANES)]
        for ref in parts:
            stats.append(decode(ref[:, :, at].astype(jnp.float32).reshape(r, LANES)))
        top = functools.reduce(jnp.maximum, stats)
        factor = [jnp.exp2(s - top) for s in stats]
        mass = sum(pltpu.roll(f, HALF, 1) * s for f, s in zip(factor, stats))
        if last:
            inverse = pltpu.roll(1.0 / jnp.where(lane < HALF, 1.0, mass), LANES - HALF, 1)
            factor = [f * inverse for f in factor]
        for h in range(sizes[j]):
            here = pl.ds(packed(j, h), HD)
            total = acc[pl.ds(first, count), :, here].reshape(r, HD) * factor[0][:, h : h + 1]
            for f, ref in zip(factor[1:], parts):
                total = total + ref[:, :, here].astype(jnp.float32).reshape(r, HD) * f[:, h : h + 1]
            if last:
                o_ref[:, pl.ds(starts[j] + h * HD, HD)] = total.astype(jnp.bfloat16)
            else:
                acc[pl.ds(first, count), :, here] = total.reshape(count, tok, HD)
        if not last:
            fused = jnp.where(lane < HALF, top, jnp.where(lane < 2 * HALF, mass, 0.0))
            acc[pl.ds(first, count), :, at] = fused.reshape(count, tok, LANES)

    def scatter_c(j):
        return [
            remote(
                send_c.at[k, :, :, wcols(j)], recv_c.at[k, :, :, wcols(j)], 5, rr_sem.at[j, 2],
                devices[na + nb + k],
            )
            for k in range(nc)
        ]

    def scatter_b(j):
        return [
            remote(
                send_b.at[k, :, :, wcols(j)], recv_b.at[k, :, :, wcols(j)], 4, rr_sem.at[j, 1],
                devices[na + k],
            )
            for k in range(nb)
        ]

    def scatter_a(j):
        return [
            remote(
                send_a.at[k, :, :, wcols(j)], recv_a.at[k, :, :, wcols(j)], 3, rr_sem.at[j, 0],
                devices[k],
            )
            for k in range(na)
        ]

    def stage_0(j):
        for source in range(1, fa):
            gather_a(j)[source - 1].wait_recv()
            for copy in gather_b(j, source):
                copy.start()
        for copy in gather_c(j, 0):
            copy.start()

    def stage_1(j):
        for column in range(1, fb):
            arrived(qall.at[pl.ds(0, fa), :, cols(j)], gb_sem.at[j, column - 1])
            for copy in gather_c(j, column):
                copy.start()

    def stage_2(j):
        for g, (low, _) in enumerate(groups):
            if nc and low == j:
                arrived(qall.at[pl.ds(0, nc * fa * fb), :, cols(g)], gc_sem.at[g])
        compute(j)
        for k, copy in enumerate(scatter_c(j)):
            pack(slot(0, 0, c_peers[k]), fa * fb, send_c.at[k], j)
            copy.start()

    def from_c(column):
        return [recv_c.at[k, pl.ds(column * fa, fa)] for k in range(nc)]

    def stage_3(j):
        if nc:
            arrived(recv_c.at[:, :, :, wcols(j)], rr_sem.at[j, 2])
        for k, copy in enumerate(scatter_b(j)):
            merge(slot(0, b_peers[k], c), fa, from_c(b_peers[k]), j)
            pack(slot(0, b_peers[k], c), fa, send_b.at[k], j)
            copy.start()

    def stage_4(j):
        if nb:
            arrived(recv_b.at[:, :, :, wcols(j)], rr_sem.at[j, 1])
        merge(slot(0, b, c), fa, from_c(b) + [recv_b.at[k] for k in range(nb)], j)
        for k, copy in enumerate(scatter_a(j)):
            pack(slot(a_peers[k], b, c), 1, send_a.at[k], j)
            copy.start()

    def stage_5(j):
        if na:
            arrived(recv_a.at[:, :, :, wcols(j)], rr_sem.at[j, 0])
        merge(own_slot, 1, [recv_a.at[k] for k in range(na)], j, last=True)

    stages = (stage_0, stage_1, stage_2, stage_3, stage_4, stage_5)
    for number, j in order_of(chunks, len(groups)):
        stages[number](j)
    for k, (count, ref) in enumerate((
        (na, qall.at[pl.ds(0, na)]),
        (nb, qall.at[pl.ds(0, fa * nb)]),
        (nc, qall.at[pl.ds(0, fa * fb * nc)]),
        (na, send_a), (nb, send_b), (nc, send_c),
    )):
        if count:
            arrived(ref, send_sem.at[k])


def per_device(queries, new_keys, new_values, cache_keys, cache_values, victims):
    members = lax.axis_size("seq")
    dims = fa, fb, fc = factors(members)
    tok, columns = queries.shape
    heads = columns // HD
    sizes = chunks_of(heads)
    chunks = len(sizes)
    parts = len(groups_of(chunks))
    rows = cache_keys.shape[0]
    keys = rows + -(-2 * tok // LANES) * LANES
    total = columns + chunks * LANES
    bf16 = jnp.bfloat16
    vmem = pl.BlockSpec(memory_space=pltpu.VMEM)
    hbm = pl.BlockSpec(memory_space=pl.ANY)
    return pl.pallas_call(
        functools.partial(kernel, dims, sizes),
        out_shape=pltpu.VMEM((tok, columns), bf16),
        in_specs=[hbm] * 6,
        out_specs=vmem,
        scratch_shapes=[
            pltpu.VMEM((tok, columns), bf16),
            pltpu.VMEM((tok, columns), bf16),
            pltpu.VMEM((1, victims.shape[0]), jnp.int32),
            pltpu.VMEM((members, tok, columns), bf16),
            pltpu.VMEM((keys, columns), bf16),
            pltpu.VMEM((keys, columns), bf16),
            pltpu.VMEM((keys, LANES), bf16),
            pltpu.VMEM((members, tok, total), jnp.float32),
            pltpu.VMEM((max(1, fc - 1), fa * fb, tok, total), bf16),
            pltpu.VMEM((max(1, fc - 1), fa * fb, tok, total), bf16),
            pltpu.VMEM((max(1, fb - 1), fa, tok, total), bf16),
            pltpu.VMEM((max(1, fb - 1), fa, tok, total), bf16),
            pltpu.VMEM((max(1, fa - 1), 1, tok, total), bf16),
            pltpu.VMEM((max(1, fa - 1), 1, tok, total), bf16),
            pltpu.SemaphoreType.DMA((2,)),
            pltpu.SemaphoreType.DMA((4,)),
            pltpu.SemaphoreType.DMA((6,)),
            pltpu.SemaphoreType.DMA((parts, max(1, fa - 1))),
            pltpu.SemaphoreType.DMA((parts, max(1, fb - 1))),
            pltpu.SemaphoreType.DMA((parts,)),
            pltpu.SemaphoreType.DMA((chunks, 3)),
        ],
        compiler_params=pltpu.CompilerParams(
            collective_id=0, has_side_effects=True, vmem_limit_bytes=60 * 1024 * 1024
        ),
    )(queries, new_keys, new_values, victims.reshape(1, -1), cache_keys, cache_values)


def solution(mesh):
    row = P(("groups", "seq"), None)
    return jax.shard_map(
        per_device,
        mesh=mesh,
        in_specs=(row, row, row, row, row, P("groups")),
        out_specs=row,
        check_vma=False,
    )
```
